256 devices in a mesh: gz: 64 (over y, z, core), gy: 4 (over x).
Axes of the slice: x: 4, y: 4, z: 8, core: 2. Of those that a mesh axis runs over, the one named last changes fastest.
Arguments:
- block: float32 [8, 512, 128, 256], P(None, 'gz', 'gy'), may hold values from -6 to 6
- conduct: float32 [512, 128, 256], P('gz', 'gy'), may hold values from 0.5 to 2
Outputs:
- basis: float32 [8, 512, 128, 256], P(None, 'gz', 'gy')
The draws below stay inside these ranges and needn't reach their ends.
All inputs are finite; a program needn't handle non-finite values.
Results may differ from the reference program's by a relative error of at most 0.00021.
Values sent between devices are 32-bit elements; how exact they have to be, the bound alone decides.
No kernel may reach another device: no remote copies, remote signals or barrier semaphores. Data moves between devices by JAX's collectives and lax.ppermute only.
A program may use at most 128 MiB of HBM per device.

```python
import math
import jax
import jax.numpy as jnp
from jax import lax

VEC = 8
DEG = 4
NX = 256
NY = 128
NZ = 512


def steps_of(rng, shape, pieces, low, high):
    gain, own = 1.0, jax.random.fold_in(rng, 6)
    for position, shards_of in pieces:
        steps = jnp.exp(jax.random.uniform(jax.random.fold_in(own, position), (shards_of,), jnp.float32, low / len(pieces), high / len(pieces)))
        gain = gain * jnp.repeat(steps, shape[position] // shards_of).reshape([-1 if axis == position else 1 for axis in range(len(shape))])
    return gain


def gaussian(stream_key, extent, width, reach, split=(), held_as=jnp.bfloat16):
    result = jax.random.normal(stream_key, extent, jnp.float32) * width
    if len(split) > 0:
        result = steps_of(stream_key, extent, split, -0.22, 0.18) * result
    return jnp.clip(result, min=-reach, max=reach).astype(held_as)


def setup_inputs(seed: int = 0) -> dict:
    key_of = jax.random.split(jax.random.key(seed), 3)
    return {
        "block": gaussian(key_of[0], (VEC, NZ, NY, NX), 1.0, 6.0, ((1, 64), (2, 4)), jnp.float32),
        "conduct": jnp.clip(jnp.exp(math.log(2.0) - 1.3862944 * jax.random.uniform(key_of[1], (NZ, NY, NX), jnp.float32) ** steps_of(key_of[1], (NZ, NY, NX), ((0, 64), (1, 4)), -0.2, 0.2)), 0.5, 2.0),
    }


mid_point = 12.75
half_width = 11.25

def stencil(padded, kpadded):
    inner = slice(1, -1)
    centre = padded[:, 1:-1, 1:-1, 1:-1]
    kcentre = kpadded[1:-1, 1:-1, 1:-1]
    shifts = [(slice(2, None), inner, inner), (slice(None, -2), inner, inner), (inner, slice(2, None), inner), (inner, slice(None, -2), inner), (inner, inner, slice(2, None)), (inner, inner, slice(None, -2))]
    total = jnp.zeros_like(centre)
    for where in shifts:
        total = total + 0.5 * (kcentre + kpadded[where]) * (centre - padded[(slice(None),) + where])
    return total

def operate(field, conduct):
    padded = jnp.pad(field, ((0, 0), (1, 1), (1, 1), (1, 1)))
    kpadded = jnp.pad(conduct, 1)
    return stencil(padded, kpadded)

def reference(block, conduct):
    field = block
    for passes in range(2):
        previous = field
        current = (operate(field, conduct) - mid_point * field) / half_width
        for step in range(DEG - 1):
            nextone = 2.0 * (operate(current, conduct) - mid_point * current) / half_width - previous
            previous = current
            current = nextone
        field = current
    vectors = field.shape[0]
    flat = field.reshape(vectors, -1)
    gram = jnp.dot(flat, flat.T, precision=lax.Precision.HIGHEST)
    lower = jnp.linalg.cholesky(gram)
    inverse = lax.linalg.triangular_solve(lower, jnp.eye(vectors, dtype=jnp.float32), left_side=True, lower=True)
    scaled = jnp.dot(inverse, flat, precision=lax.Precision.HIGHEST) * math.sqrt(flat.shape[1])
    return scaled.reshape(field.shape)
```

```python
import functools
import math

import jax
import jax.numpy as jnp
from jax import lax
from jax.experimental import pallas as pl
from jax.experimental.pallas import tpu as pltpu
from jax.sharding import PartitionSpec as P

mid_point = 12.75
half_width = 11.25
F32 = jnp.float32
H = 4


def call(kernel, outs, args, smem=0, scratch=(), flops=0, limit=40 << 20, name=None):
    specs = [pl.BlockSpec(memory_space=pltpu.SMEM)] * smem
    specs += [pl.BlockSpec(memory_space=pltpu.VMEM)] * (len(args) - smem)
    moved = sum(4 * math.prod(a.shape) for a in args) + sum(4 * math.prod(s) for s in outs)
    return pl.pallas_call(
        kernel,
        out_shape=[jax.ShapeDtypeStruct(s, F32) for s in outs],
        in_specs=specs,
        out_specs=[pl.BlockSpec(memory_space=pltpu.VMEM)] * len(outs),
        scratch_shapes=list(scratch),
        compiler_params=pltpu.CompilerParams(vmem_limit_bytes=limit),
        cost_estimate=pl.CostEstimate(flops=flops, bytes_accessed=moved, transcendentals=0),
        name=name,
    )(*args)


def turn_kernel(where, x_ref, k_ref, v_ref, c_ref, d_ref, *halves, nz, ny):
    vectors = v_ref.shape[2]
    stride = nz * ny

    half = halves[0].shape[1]

    def split(i, _):
        for part, half_ref in enumerate(halves):
            half_ref[pl.ds(8 * i, 8), :] = x_ref[pl.ds(8 * i, 8), pl.ds(part * half, half)]
        return 0

    lax.fori_loop(0, vectors * stride // 8, split, 0, unroll=8)

    def row(i, _):
        for part, half_ref in enumerate(halves):
            v_ref[i // ny, i % ny, :, pl.ds(part * half, half)] = half_ref[pl.ds(i, vectors, stride=stride), :]
        return 0

    lax.fori_loop(0, nz * ny, row, 0, unroll=8)
    c0, d0 = where[0], where[1]
    for z in range(nz):
        for j in range(H):
            c_ref[z * H + j] = v_ref[z, c0 + j]
            d_ref[z * H + j] = v_ref[z, d0 + j]
    base = nz * H
    for z in range(nz):
        row8 = z * H
        low, high = k_ref[z, :H, :], k_ref[z, ny - H :, :]
        c_ref[base + row8 // 8, pl.ds(row8 % 8, H), :] = jnp.where(c0 == 0, low, high)
        d_ref[base + row8 // 8, pl.ds(row8 % 8, H), :] = jnp.where(c0 == 0, high, low)


def faces_kernel(where, v_ref, *rest, nz, ny, first):
    if first:
        k_ref, cr_ref, dr_ref, a_ref, b_ref, kp_ref = rest
    else:
        cr_ref, dr_ref, a_ref, b_ref = rest
    c1, d1 = where[2], where[3]
    wide = ny + 2 * H
    for out_ref, z0 in ((a_ref, where[4]), (b_ref, where[5])):
        for z in range(H):
            for j in range(H):
                out_ref[z * wide + c1 + j] = cr_ref[(z0 + z) * H + j]
                out_ref[z * wide + d1 + j] = dr_ref[(z0 + z) * H + j]

            def row(y, _, z=z, z0=z0, out_ref=out_ref):
                out_ref[z * wide + H + y] = v_ref[z0 + z, y]
                return 0

            lax.fori_loop(0, ny, row, 0, unroll=8)
    if first:
        base = nz * H
        for z in range(nz):
            kp_ref[z, pl.ds(H, ny), :] = k_ref[z]
            row8 = z * H
            kc = cr_ref[base + row8 // 8, pl.ds(row8 % 8, H), :]
            kd = dr_ref[base + row8 // 8, pl.ds(row8 % 8, H), :]
            kp_ref[z, :H, :] = jnp.where(c1 == 0, kc, kd)
            kp_ref[z, ny + H :, :] = jnp.where(c1 == 0, kd, kc)
        for out_ref, z0 in ((a_ref, where[4]), (b_ref, where[5])):
            for z in range(H):
                for g in range(wide // 8):
                    out_ref[H * wide + z * (wide // 8) + g] = kp_ref[z0 + z, pl.ds(8 * g, 8), :]


def fill_kernel_fields(where, v_ref, cr_ref, dr_ref, ar_ref, br_ref, p_ref, *, nz, ny):
    wide = ny + 2 * H
    c1, d1, a1, b1 = where[2], where[3], where[6], where[7]
    for z in range(nz):
        for j in range(H):
            p_ref[H + z, c1 + j] = cr_ref[z * H + j]
            p_ref[H + z, d1 + j] = dr_ref[z * H + j]

    def own(y, _):
        for z in range(nz):
            p_ref[H + z, H + y] = v_ref[z, y]
        return 0

    lax.fori_loop(0, ny, own, 0, unroll=2)

    def halo(y, _):
        for z in range(H):
            p_ref[a1 + z, y] = ar_ref[z * wide + y]
            p_ref[b1 + z, y] = br_ref[z * wide + y]
        return 0

    lax.fori_loop(0, wide, halo, 0, unroll=2)


def coefficients(where, kp_ref, ar_ref, br_ref, ke_ref, coef, *, nz, ny):
    diag_ref, wz_ref, wy_ref, wx_ref = coef
    wide, deep = ny + 2 * H, nz + 2 * H
    tall = wide // 8
    a1, b1 = where[6], where[7]
    scale = 1.0 / half_width
    zero = jnp.zeros((8, ke_ref.shape[2]), F32)
    for z in range(deep):
        ke_ref[z, pl.ds(0, 8), :] = zero
        ke_ref[z, pl.ds(8 + wide, 8), :] = zero
    for z in range(nz):
        ke_ref[H + z, pl.ds(8, wide), :] = kp_ref[z] * scale
    for z in range(H):
        for g in range(tall):
            ke_ref[a1 + z, pl.ds(8 + 8 * g, 8), :] = ar_ref[H * wide + z * tall + g] * scale
            ke_ref[b1 + z, pl.ds(8 + 8 * g, 8), :] = br_ref[H * wide + z * tall + g] * scale
    width = ke_ref.shape[2]
    last = lax.broadcasted_iota(jnp.int32, (8, width), 1) == width - 1
    first = lax.broadcasted_iota(jnp.int32, (8, width), 1) == 0

    def one(z, _):
        below, above = jnp.maximum(z - 1, 0), jnp.minimum(z + 1, deep - 1)
        for g in range(tall):
            at = 8 + 8 * g
            k = ke_ref[z, pl.ds(at, 8), :]
            kd = ke_ref[below, pl.ds(at, 8), :]
            ku = ke_ref[above, pl.ds(at, 8), :]
            ks = ke_ref[z, pl.ds(at - 1, 8), :]
            kn = ke_ref[z, pl.ds(at + 1, 8), :]
            kl = jnp.where(last, 0.0, pltpu.roll(k, width - 1, 1))
            kr = jnp.where(first, 0.0, pltpu.roll(k, 1, 1))
            inside = k > 0
            rows = pl.ds(8 * g, 8)
            total = 6.0 * k + (((kd + ku) + (ks + kn)) + (kl + kr))
            diag_ref[z, rows, :] = jnp.where(inside, total - 2.0 * mid_point / half_width, 0.0)
            wz_ref[z, rows, :] = jnp.where(inside & (ku > 0), k + ku, 0.0)
            wy_ref[z, rows, :] = jnp.where(inside & (kn > 0), k + kn, 0.0)
            wx_ref[z, rows, :] = jnp.where(inside & ~last, k + kl, 0.0)
        return 0

    lax.fori_loop(0, deep, one, 0)


def sweep(coef, now_ref, old_ref, store, z0, zcount, y0, ycount, first):
    diag_ref, wz_ref, wy_ref, wx_ref = coef
    width = now_ref.shape[3]

    def row(i, _):
        y = y0 + i
        below = now_ref[z0 - 1, y]
        here = now_ref[z0, y]
        wbelow = wz_ref[z0 - 1, pl.ds(y, 1), :]
        for n in range(zcount):
            z = z0 + n
            above = now_ref[z + 1, y]
            wabove = wz_ref[z, pl.ds(y, 1), :]
            wx = wx_ref[z, pl.ds(y, 1), :]
            pulled = wabove * above + wbelow * below
            pulled += wy_ref[z, pl.ds(y, 1), :] * now_ref[z, y + 1] + wy_ref[z, pl.ds(y - 1, 1), :] * now_ref[z, y - 1]
            pulled += wx * pltpu.roll(here, width - 1, 1) + pltpu.roll(wx * here, 1, 1)
            image = diag_ref[z, pl.ds(y, 1), :] * here - pulled
            store(z, y, 0.5 * image if first else image - old_ref[z, y])
            below, here, wbelow = here, above, wabove
        return 0

    lax.fori_loop(0, ycount, row, 0)


def pass_steps(coef, p_ref, q_ref, last_store, *, nz, ny):
    def into(ref):
        def store(z, y, value):
            ref[z, y] = value

        return store

    for step in range(H):
        h = H - 1 - step
        now, old = (p_ref, q_ref) if step % 2 == 0 else (q_ref, p_ref)
        store = last_store if step == H - 1 else into(old)
        sweep(coef, now, old, store, H - h, nz + 2 * h, H - h, ny + 2 * h, step == 0)


def first_pass_kernel(where, v_ref, kp_ref, cr_ref, dr_ref, ar_ref, br_ref, *rest, nz, ny):
    out_ref, c_ref, d_ref = rest[:3]
    coef, (p_ref, q_ref, ke_ref) = rest[3:7], rest[7:]
    coefficients(where, kp_ref, ar_ref, br_ref, ke_ref, coef, nz=nz, ny=ny)
    fill_kernel_fields(where, v_ref, cr_ref, dr_ref, ar_ref, br_ref, p_ref, nz=nz, ny=ny)

    def store(z, y, value):
        out_ref[z - H, y - H] = value

    pass_steps(coef, p_ref, q_ref, store, nz=nz, ny=ny)
    c0, d0 = where[0], where[1]
    for z in range(nz):
        for j in range(H):
            c_ref[z * H + j] = out_ref[z, c0 + j]
            d_ref[z * H + j] = out_ref[z, d0 + j]


def second_pass_kernel(where, v_ref, cr_ref, dr_ref, ar_ref, br_ref, *rest, nz, ny):
    coef, (*f_refs, g_ref, p_ref, q_ref) = rest[:4], rest[4:]
    fill_kernel_fields(where, v_ref, cr_ref, dr_ref, ar_ref, br_ref, p_ref, nz=nz, ny=ny)
    vectors = v_ref.shape[2]
    stride = nz * ny
    half = f_refs[0].shape[1]

    def store(z, y, value):
        for part, f_ref in enumerate(f_refs):
            f_ref[pl.ds((z - H) * ny + (y - H), vectors, stride=stride), :] = value[:, part * half : (part + 1) * half]

    pass_steps(coef, p_ref, q_ref, store, nz=nz, ny=ny)
    eight = stride // 8
    pairs = [(v, w) for v in range(vectors) for w in range(v + 1)]

    def products(i, sums):
        out = list(sums)
        for f_ref in f_refs:
            rows = [f_ref[pl.ds(v * stride + i * 8, 8), :] for v in range(vectors)]
            for n, (v, w) in enumerate(pairs):
                out[n] = out[n] + rows[v] * rows[w]
        return tuple(out)

    sums = lax.fori_loop(0, eight, products, tuple(jnp.zeros((8, half), F32) for _ in pairs))
    row_of = lax.broadcasted_iota(jnp.int32, (vectors, vectors), 0)
    col_of = lax.broadcasted_iota(jnp.int32, (vectors, vectors), 1)
    gram = jnp.zeros((vectors, vectors), F32)
    for n, (v, w) in enumerate(pairs):
        value = jnp.sum(sums[n])
        here = ((row_of == v) & (col_of == w)) | ((row_of == w) & (col_of == v))
        gram = jnp.where(here, value, gram)
    g_ref[...] = gram


def basis_kernel(w_ref, *rest, cells):
    *f_refs, out_ref = rest
    vectors = w_ref.shape[0]
    half = f_refs[0].shape[1]

    def rows(i, _):
        for part, f_ref in enumerate(f_refs):
            cols = pl.ds(part * half, half)
            have = [f_ref[pl.ds(v * cells + i * 8, 8), :] for v in range(vectors)]
            for v in range(vectors):
                total = w_ref[v, 0] * have[0]
                for w in range(1, v + 1):
                    total = total + w_ref[v, w] * have[w]
                out_ref[pl.ds(v * cells + i * 8, 8), cols] = total
        return 0

    lax.fori_loop(0, cells // 8, rows, 0)


def swaps(payloads, perms):
    return [lax.ppermute(p, axis, pairs) for p, (axis, pairs) in zip(payloads, perms)]


def shards(block, conduct):
    vectors, nz, ny, nx = block.shape
    zcount, ycount = lax.axis_size("gz"), lax.axis_size("gy")
    zi, yi = lax.axis_index("gz"), lax.axis_index("gy")
    a_pairs = ("gz", [(i, i ^ 1) for i in range(zcount)])
    b_pairs = ("gz", [(i, ((i + 1) ^ 1) - 1) for i in range(1, zcount - 1)])
    c_pairs = ("gy", [(i, i ^ 1) for i in range(ycount)])
    d_pairs = ("gy", [(i, ((i + 1) ^ 1) - 1) for i in range(1, ycount - 1)])
    zodd, yodd = zi % 2, yi % 2
    where = jnp.stack([
        (1 - yodd) * (ny - H), yodd * (ny - H),
        (1 - yodd) * (ny + H), yodd * (ny + H),
        (1 - zodd) * (nz - H), zodd * (nz - H),
        (1 - zodd) * (nz + H), zodd * (nz + H),
    ]).astype(jnp.int32)
    wide, deep = ny + 2 * H, nz + 2 * H
    row = (vectors, nx)
    yface, zface = (nz * H, *row), (H * wide, *row)
    sizes = dict(nz=nz, ny=ny)

    def part(kernel, **more):
        return functools.partial(kernel, **sizes, **more)

    ext = pltpu.VMEM((deep, wide, *row), F32)
    field = (nz, ny, *row)
    coefs = [(deep, wide, nx)] * 4

    with jax.named_scope("turn"):
        extra = nz * H // 8
        v, c, d = call(part(turn_kernel), [field, (nz * H + extra, *row), (nz * H + extra, *row)],
                       (where, block.reshape(vectors * nz * ny, nx), conduct), smem=1,
                       scratch=[pltpu.VMEM((vectors * nz * ny, nx // 2), F32)] * 2, name="turn")
    c, d = swaps((c, d), (c_pairs, d_pairs))
    zrows = H * wide + H * wide // 8
    a, b, kp = call(part(faces_kernel, first=True), [(zrows, *row), (zrows, *row), (nz, wide, nx)],
                    (where, v, conduct, c, d), smem=1, name="faces0")
    a, b = swaps((a, b), (a_pairs, b_pairs))
    flops = 16 * vectors * nx * deep * wide * H
    v, c, d, *coef = call(part(first_pass_kernel), [field, yface, yface, *coefs], (where, v, kp, c, d, a, b), smem=1,
                          scratch=[ext, ext, pltpu.VMEM((deep, wide + 16, nx), F32)], flops=flops, name="pass0")
    c, d = swaps((c, d), (c_pairs, d_pairs))
    a, b = call(part(faces_kernel, first=False), [zface, zface], (where, v, c, d), smem=1, name="faces1")
    a, b = swaps((a, b), (a_pairs, b_pairs))
    *f, gram = call(part(second_pass_kernel), [(vectors * nz * ny, nx // 2)] * 2 + [(vectors, vectors)],
                   (where, v, c, d, a, b, *coef), smem=1, scratch=[ext, ext], flops=flops, name="pass1")
    gram = sum_everywhere(gram, zcount, ycount)
    lower = jnp.linalg.cholesky(gram)
    inverse = lax.linalg.triangular_solve(lower, jnp.eye(vectors, dtype=F32), left_side=True, lower=True)
    inverse = inverse * math.sqrt(nx * ny * nz * zcount * ycount)
    (out,) = call(functools.partial(basis_kernel, cells=nz * ny), [(vectors * nz * ny, nx)], (inverse, *f), smem=1, name="basis")
    return out.reshape(block.shape)


def sum_everywhere(part, zcount, ycount):
    part = part + lax.ppermute(part, "gz", [(i, i ^ 1) for i in range(zcount)])
    line = 8
    planes = zcount // (2 * line)

    def flat(y, x, z, core):
        return ((y * line + z) * 2 + core) * ycount + x

    planar = [[flat(y, x, z, core) for y in range(planes) for x in range(ycount)] for z in range(line) for core in range(2)]
    part = everyone(part, ("gz", "gy"), planar)
    lines = [[(y * line + z) * 2 + core for z in range(line)] for y in range(planes) for core in range(2)]
    return everyone(part, "gz", lines)


def everyone(part, axes, groups):
    n = len(groups[0])
    copies = jnp.broadcast_to(part[None], (n, *part.shape))
    return jnp.sum(lax.all_to_all(copies, axes, 0, 0, axis_index_groups=groups, tiled=True), axis=0)


def solution(mesh):
    in_specs = (P(None, "gz", "gy", None), P("gz", "gy", None))
    out_specs = P(None, "gz", "gy", None)
    return jax.shard_map(shards, mesh=mesh, in_specs=in_specs, out_specs=out_specs, check_vma=False)
```

```python
import functools
import math

import jax
import jax.numpy as jnp
from jax import lax
from jax.experimental import pallas as pl
from jax.experimental.pallas import tpu as pltpu
from jax.sharding import PartitionSpec as P


mid_point = 12.75
half_width = 11.25
F32 = jnp.float32
H = 4
COEFS = 4
GROUPS = (4, 4)
PAD = 8

C_FROM, D_FROM, A_FROM, B_FROM = range(4)
C_TO, D_TO, A_TO, _ = range(4, 8)
Z_ODD = 8

CORNER = [(dz, dy, high) for dz in range(1, H) for dy in range(1, H - dz + 1) for high in (0, 1)]


def call(kernel, outs, args, alias=None, scratch=(), flops=0, limit=16 << 20, space=pltpu.VMEM):
    specs = [pl.BlockSpec(memory_space=pltpu.SMEM)]
    specs += [pl.BlockSpec(memory_space=space)] * (len(args) - 1)
    return pl.pallas_call(
        kernel,
        out_shape=[jax.ShapeDtypeStruct(s, F32) for s in outs],
        in_specs=specs,
        out_specs=[pl.BlockSpec(memory_space=pltpu.VMEM)] * len(outs),
        scratch_shapes=list(scratch),
        input_output_aliases=alias or {},
        compiler_params=pltpu.CompilerParams(vmem_limit_bytes=limit),
        cost_estimate=pl.CostEstimate(flops=flops, bytes_accessed=1 << 16, transcendentals=0),
    )(*args)


def halves(value):
    width = value.shape[-1] // 2
    return value[..., :width], value[..., width:]


def lanes():
    return lax.broadcasted_iota(jnp.int32, (8, 128), 1)


def even_first(back=False):
    row, col = (lax.broadcasted_iota(jnp.int32, (256, 256), axis) for axis in ((1, 0) if back else (0, 1)))
    return jnp.where(row == 2 * (col % 128) + col // 128, 1.0, 0.0).astype(jnp.bfloat16)


def permuted(value, matrix, terms=3):
    total = None
    for term in range(terms):
        high = value.astype(jnp.bfloat16)
        moved = jnp.dot(high, matrix, preferred_element_type=F32)
        total = moved if total is None else total + moved
        if term + 1 < terms:
            value = value - high.astype(F32)
    return total


def cut_faces(where, p_ref, faces, *, nz, ny):
    a_ref, b_ref, c_ref, d_ref = faces

    def row(y, _):
        for out_ref, start in ((a_ref, where[A_FROM]), (b_ref, where[B_FROM])):
            for z in range(H):
                out_ref[z * ny + y] = p_ref[H + start + z, H + y]
        return 0

    lax.fori_loop(0, ny, row, 0, unroll=2)
    for out_ref, start in ((c_ref, where[C_FROM]), (d_ref, where[D_FROM])):
        def layer(z, _, out_ref=out_ref, start=start):
            for j in range(H):
                out_ref[z * H + j] = p_ref[H + z, H + start + j]
            return 0

        lax.fori_loop(0, nz, layer, 0, unroll=2)


def turn_kernel(where, x_ref, k_ref, p_ref, ke_ref, *rest, nz, ny):
    faces, (k_here, sems, k_sem) = rest[:4], rest[4:]
    a_ref, b_ref, c_ref, d_ref = faces
    vectors = p_ref.shape[2]
    k_copy = pltpu.make_async_copy(k_ref, k_here, k_sem)
    copies = [
        pltpu.make_async_copy(x_ref.at[v], p_ref.at[pl.ds(H, nz), pl.ds(H, ny), v, :], sems.at[v]) for v in range(vectors)
    ]
    k_copy.start()
    for copy in copies:
        copy.start()
    k_copy.wait()
    matrix = even_first()
    nx = p_ref.shape[3]
    k_turned = permuted(k_here[...].reshape(nz * ny, nx) * (1.0 / half_width), matrix)
    for z in range(nz):
        ke_ref[H + z, pl.ds(PAD + H, ny), :] = k_turned[z * ny : (z + 1) * ny]
    for copy in copies:
        copy.wait()

    for z in range(0, nz, 4):
        block = p_ref.at[pl.ds(H + z, 4), pl.ds(H, ny)]
        block[...] = permuted(block[...].reshape(4 * ny * vectors, nx), matrix).reshape(4, ny, vectors, nx)
    cut_faces(where, p_ref, faces, nz=nz, ny=ny)
    c_low = where[C_FROM] == 0
    for z in range(nz):
        low, high = ke_ref[H + z, pl.ds(PAD + H, H), :], ke_ref[H + z, pl.ds(PAD + ny, H), :]
        at = nz * H + z * H // 8
        c_ref[at, pl.ds(z * H % 8, H), :] = jnp.where(c_low, low, high)
        d_ref[at, pl.ds(z * H % 8, H), :] = jnp.where(c_low, high, low)
    for z in range(H):
        for g in range(ny // 8):
            for out_ref, start in ((a_ref, where[A_FROM]), (b_ref, where[B_FROM])):
                out_ref[H * ny + z * (ny // 8) + g] = ke_ref[H + start + z, pl.ds(PAD + H + 8 * g, 8), :]


def own_layer(where, side, dz, nz):
    low = where[Z_ODD] == 1 - side
    return jnp.where(low, dz - 1, nz - dz)


def halo_layer(where, side, dz, nz):
    low = where[Z_ODD] == 1 - side
    return jnp.where(low, H - dz, H + nz + dz - 1)


def halo_row(dy, high, ny):
    return H + ny + dy - 1 if high else H - dy


def corner_kernel(where, p_in, *rest, nz, ny, first):
    if first:
        _, cr_ref, dr_ref, p_ref, ke_ref, a_ref, b_ref = rest
    else:
        cr_ref, dr_ref, p_ref, a_ref, b_ref = rest

    def layer(z, _):
        for j in range(H):
            p_ref[H + z, where[C_TO] + j] = cr_ref[z * H + j]
            p_ref[H + z, where[D_TO] + j] = dr_ref[z * H + j]
        return 0

    lax.fori_loop(0, nz, layer, 0, unroll=2)
    for side, out_ref in enumerate((a_ref, b_ref)):
        for n, (dz, dy, high) in enumerate(CORNER):
            out_ref[n] = p_ref[H + own_layer(where, side, dz, nz), halo_row(dy, high, ny)]
    if first:
        c_low = where[C_TO] == 0
        for z in range(nz):
            at = nz * H + z * H // 8
            kc, kd = cr_ref[at, pl.ds(z * H % 8, H), :], dr_ref[at, pl.ds(z * H % 8, H), :]
            ke_ref[H + z, pl.ds(PAD, H), :] = jnp.where(c_low, kc, kd)
            ke_ref[H + z, pl.ds(PAD + H + ny, H), :] = jnp.where(c_low, kd, kc)
        for side, out_ref in enumerate((a_ref, b_ref)):
            for n, (dz, dy, high) in enumerate(CORNER):
                row = ke_ref[H + own_layer(where, side, dz, nz), pl.ds(PAD + halo_row(dy, high, ny), 1), :]
                out_ref[len(CORNER) + n // 8, pl.ds(n % 8, 1), :] = row


def fill_side(where, side, p_ref, ke_ref, face_ref, corner_ref, *, nz, ny):
    start = where[A_TO + side]

    def row(y, _):
        for z in range(H):
            p_ref[start + z, H + y] = face_ref[z * ny + y]
        return 0

    lax.fori_loop(0, ny, row, 0, unroll=4)
    for n, (dz, dy, high) in enumerate(CORNER):
        p_ref[halo_layer(where, side, dz, nz), halo_row(dy, high, ny)] = corner_ref[n]
    if ke_ref is not None:
        for z in range(H):
            for g in range(ny // 8):
                ke_ref[start + z, pl.ds(PAD + H + 8 * g, 8), :] = face_ref[H * ny + z * (ny // 8) + g]
        for n, (dz, dy, high) in enumerate(CORNER):
            row = corner_ref[len(CORNER) + n // 8, pl.ds(n % 8, 1), :]
            ke_ref[halo_layer(where, side, dz, nz), pl.ds(PAD + halo_row(dy, high, ny), 1), :] = row


def coefficients(ke_ref, coef, z0, count):
    diag_ref, wz_ref, wy_ref, wx_ref = coef
    deep, wide = diag_ref.shape[0], diag_ref.shape[1]
    lane = lanes()

    def one(i, _):
        z = z0 + i
        below, above = jnp.maximum(z - 1, 0), jnp.minimum(z + 1, deep - 1)
        for g in range(wide // 8):
            at = PAD + 8 * g
            rows = pl.ds(8 * g, 8)
            k = ke_ref[z, pl.ds(at, 8), :]
            ku = ke_ref[above, pl.ds(at, 8), :]
            kn = ke_ref[z, pl.ds(at + 1, 8), :]
            around = (ke_ref[below, pl.ds(at, 8), :] + ku) + (ke_ref[z, pl.ds(at - 1, 8), :] + kn)
            inside = k > 0
            wz_ref[z, rows, :] = jnp.where(inside & (ku > 0), k + ku, 0.0)
            wy_ref[z, rows, :] = jnp.where(inside & (kn > 0), k + kn, 0.0)
            even, odd = halves(k)
            before = jnp.where(lane == 0, 0.0, pltpu.roll(odd, 1, 1))
            after = jnp.where(lane == 127, 0.0, pltpu.roll(even, 127, 1))
            even_around, odd_around = halves(around)
            shift = 2.0 * mid_point / half_width
            in_even, in_odd = even > 0, odd > 0
            diag_ref[z, rows, pl.ds(0, 128)] = jnp.where(in_even, 6.0 * even + (even_around + (before + odd)) - shift, 0.0)
            diag_ref[z, rows, pl.ds(128, 128)] = jnp.where(in_odd, 6.0 * odd + (odd_around + (even + after)) - shift, 0.0)
            wx_ref[z, rows, pl.ds(0, 128)] = jnp.where(in_even, even + odd, 0.0)
            wx_ref[z, rows, pl.ds(128, 128)] = jnp.where(in_odd & (lane < 127), odd + after, 0.0)
        return 0

    lax.fori_loop(0, count, one, 0)


def sweep(coef, now_ref, old_ref, store, z0, zcount, y0, ycount, first, group):
    diag_ref, wz_ref, wy_ref, wx_ref = coef
    both = (pl.ds(0, 128), pl.ds(128, 128))

    def rows(y, group):
        field = lambda z, y: [now_ref[z, y, :, part] for part in both]
        weight = lambda ref, z, y: halves(ref[z, pl.ds(y, 1), :])

        def across(value, weights):
            (even, odd), (inner, outer) = value, weights
            return inner * odd + pltpu.roll(outer * odd, 1, 1), inner * even + outer * pltpu.roll(even, 127, 1)

        def fetch(n):
            z = z0 + n
            return dict(
                ends=(field(z, y - 1), field(z, y + group)),
                wy=[weight(wy_ref, z, y - 1 + r) for r in range(group + 1)],
                diag=[weight(diag_ref, z, y + r) for r in range(group)],
                old=None if first else [[old_ref[z, y + r, :, part] for part in both] for r in range(group)],
            )

        below = [field(z0 - 1, y + r) for r in range(group)]
        here = [field(z0, y + r) for r in range(group)]
        wbelow = [weight(wz_ref, z0 - 1, y + r) for r in range(group)]
        sides = [across(here[r], weight(wx_ref, z0, y + r)) for r in range(group)]
        got = fetch(0)
        for n in range(zcount):
            z = z0 + n
            above = [field(z + 1, y + r) for r in range(group)]
            wabove = [weight(wz_ref, z, y + r) for r in range(group)]
            column = [got["ends"][0], *here, got["ends"][1]]
            made = []
            for r in range(group):
                for part in range(2):
                    pulled = wabove[r][part] * above[r][part] + wbelow[r][part] * below[r][part]
                    pulled += got["wy"][r + 1][part] * column[r + 2][part] + got["wy"][r][part] * column[r][part]
                    image = got["diag"][r][part] * here[r][part] - (pulled + sides[r][part])
                    made.append((r, part, 0.5 * image if first else image - got["old"][r][part]))
            if n + 1 < zcount:
                sides = [across(above[r], weight(wx_ref, z + 1, y + r)) for r in range(group)]
                got = fetch(n + 1)
            for r, part, value in made:
                store(z, y + r, part, value)
            below, here, wbelow = here, above, wabove

    def many(i, _):
        rows(y0 + group * i, group)
        return 0

    lax.fori_loop(0, ycount // group, many, 0)
    if ycount % group:
        rows(y0 + ycount - ycount % group, ycount % group)


def steps(where, side, coef, p_ref, q_ref, last_store, *, nz, ny):
    def into(ref):
        def store(z, y, part, value):
            ref[z, y, :, pl.ds(128 * part, 128)] = value

        return store

    odd = where[Z_ODD] == 1
    for step in range(1, H + 1):
        h = H - step
        now, old = (p_ref, q_ref) if step % 2 == 1 else (q_ref, p_ref)
        store = last_store if step == H and last_store is not None else into(old)
        if side == 0:
            z0, zcount = jnp.where(odd, H - h, H + step), nz + h - step
        else:
            z0, zcount = jnp.where(odd, H + nz - step, H - h), h + step
        sweep(coef, now, old, store, z0, zcount, H - h, ny + 2 * h, step == 1, GROUPS[side])


def near_kernel(where, p_in, *rest, nz, ny, first):
    size = dict(nz=nz, ny=ny)
    if first:
        ke_in, face_ref, corner_ref, p_ref, ke_ref, q_ref, *coef = rest
        store = None
    else:
        *coef, face_ref, corner_ref, p_ref, q_ref, left_ref, right_ref, g_ref = rest
        ke_ref = None
        store = filtered_store((left_ref, right_ref), **size)
    fill_side(where, 0, p_ref, ke_ref, face_ref, corner_ref, **size)
    if first:
        coefficients(ke_ref, coef, jnp.where(where[Z_ODD] == 1, 0, H), nz + H)
    steps(where, 0, coef, p_ref, q_ref, store, **size)
    if not first:
        pairs = products((left_ref, right_ref), where[A_FROM] * ny // 8, H * ny // 8, nz * ny, None)
        for n, total in enumerate(pairs):
            g_ref[n] = total


def far_kernel(where, p_in, q_in, *rest, nz, ny, first):
    size = dict(nz=nz, ny=ny)
    if first:
        ke_in, *rest = rest
        rest = rest[COEFS:]
        face_ref, corner_ref, p_ref, q_ref, ke_ref, *rest = rest
        coef, faces = rest[:COEFS], rest[COEFS:]
        store = None
    else:
        *coef, face_ref, corner_ref, left_in, right_in, pairs_ref, p_ref, q_ref, left_ref, right_ref, g_ref = rest
        ke_ref = None
        store = filtered_store((left_ref, right_ref), **size)
    fill_side(where, 1, p_ref, ke_ref, face_ref, corner_ref, **size)
    if first:
        coefficients(ke_ref, coef, jnp.where(where[Z_ODD] == 1, H + nz - 1, 0), H + 1)
    steps(where, 1, coef, p_ref, q_ref, store, **size)
    if first:
        cut_faces(where, p_ref, faces, **size)
    else:
        sums = products((left_ref, right_ref), where[B_FROM] * ny // 8, H * ny // 8, nz * ny, pairs_ref)
        row_of = lax.broadcasted_iota(jnp.int32, g_ref.shape, 0)
        col_of = lax.broadcasted_iota(jnp.int32, g_ref.shape, 1)
        gram = jnp.zeros(g_ref.shape, F32)
        for total, (v, w) in zip(sums, PAIRS):
            here = ((row_of == v) & (col_of == w)) | ((row_of == w) & (col_of == v))
            gram = jnp.where(here, jnp.sum(total), gram)
        g_ref[...] = gram


PAIRS = [(v, w) for v in range(8) for w in range(v + 1)]


def filtered_store(outs, *, nz, ny):
    def store(z, y, part, value):
        outs[part][pl.ds((z - H) * ny + (y - H), 8, stride=nz * ny), :] = value

    return store


def products(parts, start, count, cells, initial):
    def group(i, sums):
        out = list(sums)
        for ref in parts:
            rows = [ref[pl.ds(pl.multiple_of(v * cells + (start + i) * 8, 8), 8), :] for v in range(8)]
            for n, (v, w) in enumerate(PAIRS):
                out[n] = out[n] + rows[v] * rows[w]
        return tuple(out)

    zero = [jnp.zeros((8, 128), F32) if initial is None else initial[n] for n in range(len(PAIRS))]
    return lax.fori_loop(0, count, group, tuple(zero))


def basis_kernel(g_ref, even_ref, odd_ref, out_ref, w_ref, made_ref, *, scale):
    vectors = out_ref.shape[0]

    @pl.when(pl.program_id(0) == 0)
    def _():
        row = lax.broadcasted_iota(jnp.int32, (vectors, 128), 0)
        col = lax.broadcasted_iota(jnp.int32, (vectors, 128), 1)
        gram = jnp.sum(g_ref[...], axis=0)
        both = jnp.where(col < vectors, gram, jnp.where(col - vectors == row, 1.0, 0.0))
        scales = jnp.zeros((vectors, 128), F32)
        for k in range(vectors):
            pivot_row = jnp.broadcast_to(both[k : k + 1, :], both.shape)
            pivot = jnp.broadcast_to(pivot_row[:, k : k + 1], both.shape)
            scales = jnp.where(row == k, scale * lax.rsqrt(pivot), scales)
            if k + 1 < vectors:
                factor = jnp.broadcast_to(both[:, k : k + 1], both.shape) / pivot
                both = both - jnp.where(row > k, factor, 0.0) * pivot_row
        w_ref[...] = both * scales

    have = w_ref[...]
    spread = lambda v, w: jnp.broadcast_to(have[v : v + 1, vectors + w : vectors + w + 1], (8, 128))
    weights = [[spread(v, w) for w in range(v + 1)] for v in range(vectors)]
    count = out_ref.shape[1]
    first = pl.program_id(0) * count

    def combine(i, _):
        for part, ref in enumerate((even_ref, odd_ref)):
            field = [ref[v, pl.ds(pl.multiple_of(first + i * 8, 8), 8), :] for v in range(vectors)]
            for v in range(vectors):
                total = weights[v][0] * field[0]
                for w in range(1, v + 1):
                    total = total + weights[v][w] * field[w]
                made_ref[v, pl.ds(pl.multiple_of(i * 8, 8), 8), pl.ds(part * 128, 128)] = total
        return 0

    lax.fori_loop(0, count // 8, combine, 0)
    matrix = even_first(back=True)

    made = permuted(made_ref[...].reshape(vectors * count, 256), matrix, terms=2)
    out_ref[...] = made.reshape(out_ref.shape)


def basis(gram, left, right, cells, scale):
    vectors = gram.shape[1]
    blocks = 4
    rows = cells // blocks
    return pl.pallas_call(
        functools.partial(basis_kernel, scale=scale),
        grid=(blocks,),
        out_shape=jax.ShapeDtypeStruct((vectors, cells, 256), F32),
        in_specs=[pl.BlockSpec(memory_space=pltpu.VMEM)] * 3,
        out_specs=pl.BlockSpec((vectors, rows, 256), lambda i: (0, i, 0)),
        scratch_shapes=[pltpu.VMEM((vectors, 128), F32), pltpu.VMEM((vectors, rows, 256), F32)],
        compiler_params=pltpu.CompilerParams(vmem_limit_bytes=16 << 20),
        name="basis",
    )(gram, left.reshape(vectors, cells, 128), right.reshape(vectors, cells, 128))


def shards(block, conduct):
    vectors, nz, ny, nx = block.shape
    zcount, ycount = lax.axis_size("gz"), lax.axis_size("gy")
    zi, yi = lax.axis_index("gz"), lax.axis_index("gy")
    a_pairs = ("gz", [(i, i ^ 1) for i in range(zcount)])
    b_pairs = ("gz", [(i, ((i + 1) ^ 1) - 1) for i in range(1, zcount - 1)])
    c_pairs = ("gy", [(i, i ^ 1) for i in range(ycount)])
    d_pairs = ("gy", [(i, ((i + 1) ^ 1) - 1) for i in range(1, ycount - 1)])
    zodd, yodd = zi % 2, yi % 2
    where = jnp.stack([
        (1 - yodd) * (ny - H), yodd * (ny - H), (1 - zodd) * (nz - H), zodd * (nz - H),
        (1 - yodd) * (ny + H), yodd * (ny + H), (1 - zodd) * (nz + H), zodd * (nz + H), zodd,
    ]).astype(jnp.int32)
    wide, deep = ny + 2 * H, nz + 2 * H
    row = (vectors, nx)
    cells = nz * ny
    field, ke, weights = (deep, wide, *row), (deep, wide + 2 * PAD, nx), [(deep, wide, nx)] * COEFS
    halves_shape = [(vectors * cells, nx // 2)] * 2
    corner = len(CORNER)
    kernel = lambda f, **more: functools.partial(f, nz=nz, ny=ny, **more)
    swap = lambda payload, pairs: lax.ppermute(payload, *pairs)

    def exchange(p, ke, a, b, c, d):
        c = swap(c, c_pairs)
        d = swap(d, d_pairs)
        b = swap(b, b_pairs)
        a = swap(a, a_pairs)
        first = ke is not None
        n = corner + 2 if first else corner
        keep = [field] + ([ke.shape] if first else [])
        outs = keep + [(n, *row)] * 2
        args = (where, p) + ((ke,) if first else ()) + (c, d)
        alias = {1: 0, 2: 1} if first else {1: 0}
        *kept, ac, bc = call(kernel(corner_kernel, first=first), outs, args, alias)
        ac = swap(ac, a_pairs)
        bc = swap(bc, b_pairs)
        return kept, a, b, ac, bc

    near_flops, far_flops = 20_000_000, 12_000_000
    extra_z, extra_y = H * ny // 8, nz * H // 8
    p, k, a, b, c, d = call(
        kernel(turn_kernel),
        [field, ke, (H * ny + extra_z, *row), (H * ny + extra_z, *row), (nz * H + extra_y, *row), (nz * H + extra_y, *row)],
        (where, *(pltpu.with_memory_space_constraint(arg, pltpu.HBM) for arg in (block, conduct))), space=pltpu.HBM,
        scratch=[pltpu.VMEM(conduct.shape, F32), pltpu.SemaphoreType.DMA((vectors,)), pltpu.SemaphoreType.DMA])
    (p, k), a, b, ac, bc = exchange(p, k, a, b, c, d)
    p, k, q, *coef = call(kernel(near_kernel, first=True), [field, ke, field, *weights], (where, p, k, a, ac),
                          {1: 0, 2: 1}, flops=near_flops)
    p, q, k, *rest = call(
        kernel(far_kernel, first=True),
        [field, field, ke, *weights, (H * ny, *row), (H * ny, *row), (nz * H, *row), (nz * H, *row)],
        (where, p, q, k, *coef, b, bc), {n + 1: n for n in range(3 + COEFS)}, flops=far_flops)
    coef, (a, b, c, d) = rest[:COEFS], rest[COEFS:]
    (p,), a, b, ac, bc = exchange(p, None, a, b, c, d)
    p, q, left, right, pairs = call(
        kernel(near_kernel, first=False), [field, field, *halves_shape, (len(PAIRS), 8, 128)],
        (where, p, *coef, a, ac), {1: 0}, flops=near_flops)
    _, _, left, right, gram = call(
        kernel(far_kernel, first=False), [field, field, *halves_shape, (vectors, 128)],
        (where, p, q, *coef, b, bc, left, right, pairs), {1: 0, 2: 1, COEFS + 5: 2, COEFS + 6: 3}, flops=far_flops)
    gram = sum_everywhere(gram, zcount, ycount)
    out = basis(gram, left, right, cells, math.sqrt(nx * cells * zcount * ycount))
    return out.reshape(block.shape)


def sum_everywhere(part, zcount, ycount):
    part = part + lax.ppermute(part, "gz", [(i, i ^ 1) for i in range(zcount)])
    line = 8
    planes = zcount // (2 * line)

    def flat(y, x, z, core):
        return ((y * line + z) * 2 + core) * ycount + x

    planar = [[flat(y, x, z, core) for y in range(planes) for x in range(ycount)] for z in range(line) for core in range(2)]
    part = jnp.sum(gathered(part, ("gz", "gy"), planar), axis=0)
    lines = [[(y * line + z) * 2 + core for z in range(line)] for y in range(planes) for core in range(2)]
    return gathered(part, "gz", lines)


def gathered(part, axes, groups):
    n = len(groups[0])
    copies = jnp.broadcast_to(part[None], (n, *part.shape))
    return lax.all_to_all(copies, axes, 0, 0, axis_index_groups=groups, tiled=True)


def solution(mesh):
    in_specs = (P(None, "gz", "gy", None), P("gz", "gy", None))
    out_specs = P(None, "gz", "gy", None)
    return jax.shard_map(shards, mesh=mesh, in_specs=in_specs, out_specs=out_specs, check_vma=False)
```

```python
import functools
import math

import jax
import jax.numpy as jnp
from jax import lax
from jax.experimental import pallas as pl
from jax.experimental.pallas import tpu as pltpu
from jax.sharding import PartitionSpec as P


mid_point = 12.75
half_width = 11.25
F32 = jnp.float32
H = 4
COEFS = 4
CHUNK = 4
INNER_ROWS = (6, 7, 13, 12)
FAR_ROWS = (19, 12, 17, 16)
PAD = 8

C_FROM, D_FROM, A_FROM, B_FROM = range(4)
C_TO, D_TO, A_TO, _ = range(4, 8)
Z_ODD = 8

CORNER = [(dz, dy, high) for dz in range(1, H) for dy in range(1, H - dz + 1) for high in (0, 1)]


def call(kernel, outs, args, alias=None, scratch=(), flops=0, limit=16 << 20, space=pltpu.VMEM):
    specs = [pl.BlockSpec(memory_space=pltpu.SMEM)]
    specs += [pl.BlockSpec(memory_space=space)] * (len(args) - 1)
    return pl.pallas_call(
        kernel,
        out_shape=[jax.ShapeDtypeStruct(s, F32) for s in outs],
        in_specs=specs,
        out_specs=[pl.BlockSpec(memory_space=pltpu.VMEM)] * len(outs),
        scratch_shapes=list(scratch),
        input_output_aliases=alias or {},
        compiler_params=pltpu.CompilerParams(vmem_limit_bytes=limit),
        cost_estimate=pl.CostEstimate(flops=flops, bytes_accessed=1 << 16, transcendentals=0),
    )(*args)


def halves(value):
    width = value.shape[-1] // 2
    return value[..., :width], value[..., width:]


def lanes():
    return lax.broadcasted_iota(jnp.int32, (8, 128), 1)


def even_first(back=False):
    row, col = (lax.broadcasted_iota(jnp.int32, (256, 256), axis) for axis in ((1, 0) if back else (0, 1)))
    return jnp.where(row == 2 * (col % 128) + col // 128, 1.0, 0.0).astype(jnp.bfloat16)


def permuted(value, matrix, terms=3):
    total = None
    for term in range(terms):
        high = value.astype(jnp.bfloat16)
        moved = jnp.dot(high, matrix, preferred_element_type=F32)
        total = moved if total is None else total + moved
        if term + 1 < terms:
            value = value - high.astype(F32)
    return total


def cut_faces(where, p_ref, faces, *, nz, ny):
    a_ref, b_ref, c_ref, d_ref = faces

    def row(y, _):
        for out_ref, start in ((a_ref, where[A_FROM]), (b_ref, where[B_FROM])):
            for z in range(H):
                out_ref[z * ny + y] = p_ref[H + start + z, H + y]
        return 0

    lax.fori_loop(0, ny, row, 0, unroll=2)
    for out_ref, start in ((c_ref, where[C_FROM]), (d_ref, where[D_FROM])):
        def layer(z, _, out_ref=out_ref, start=start):
            for j in range(H):
                out_ref[z * H + j] = p_ref[H + z, H + start + j]
            return 0

        lax.fori_loop(0, nz, layer, 0, unroll=2)


def turn_kernel(where, x_ref, k_ref, p_ref, ke_ref, *rest, nz, ny):
    faces, (k_here, sems, k_sem) = rest[:4], rest[4:]
    a_ref, b_ref, c_ref, d_ref = faces
    vectors = p_ref.shape[2]
    k_copy = pltpu.make_async_copy(k_ref, k_here, k_sem)
    copies = [
        pltpu.make_async_copy(x_ref.at[v], p_ref.at[pl.ds(H, nz), pl.ds(H, ny), v, :], sems.at[v]) for v in range(vectors)
    ]
    k_copy.start()
    for copy in copies:
        copy.start()
    k_copy.wait()
    matrix = even_first()
    nx = p_ref.shape[3]
    k_turned = permuted(k_here[...].reshape(nz * ny, nx) * (1.0 / half_width), matrix)
    for z in range(nz):
        ke_ref[H + z, pl.ds(PAD + H, ny), :] = k_turned[z * ny : (z + 1) * ny]
    for copy in copies:
        copy.wait()
    for z in range(0, nz, CHUNK):
        block = p_ref.at[pl.ds(H + z, CHUNK), pl.ds(H, ny)]
        block[...] = permuted(block[...].reshape(CHUNK * ny * vectors, nx), matrix).reshape(CHUNK, ny, vectors, nx)
    cut_faces(where, p_ref, faces, nz=nz, ny=ny)
    c_low = where[C_FROM] == 0
    for z in range(nz):
        low, high = ke_ref[H + z, pl.ds(PAD + H, H), :], ke_ref[H + z, pl.ds(PAD + ny, H), :]
        at = nz * H + z * H // 8
        c_ref[at, pl.ds(z * H % 8, H), :] = jnp.where(c_low, low, high)
        d_ref[at, pl.ds(z * H % 8, H), :] = jnp.where(c_low, high, low)
    for z in range(H):
        for g in range(ny // 8):
            for out_ref, start in ((a_ref, where[A_FROM]), (b_ref, where[B_FROM])):
                out_ref[H * ny + z * (ny // 8) + g] = ke_ref[H + start + z, pl.ds(PAD + H + 8 * g, 8), :]


def own_layer(where, side, dz, nz):
    low = where[Z_ODD] == 1 - side
    return jnp.where(low, dz - 1, nz - dz)


def halo_layer(where, side, dz, nz):
    low = where[Z_ODD] == 1 - side
    return jnp.where(low, H - dz, H + nz + dz - 1)


def halo_row(dy, high, ny):
    return H + ny + dy - 1 if high else H - dy


def corner_kernel(where, p_in, *rest, nz, ny, first):
    if first:
        _, cr_ref, dr_ref, p_ref, ke_ref, a_ref, b_ref = rest
    else:
        cr_ref, dr_ref, p_ref, a_ref, b_ref = rest

    def layer(z, _):
        for j in range(H):
            p_ref[H + z, where[C_TO] + j] = cr_ref[z * H + j]
            p_ref[H + z, where[D_TO] + j] = dr_ref[z * H + j]
        return 0

    lax.fori_loop(0, nz, layer, 0, unroll=2)
    for side, out_ref in enumerate((a_ref, b_ref)):
        for n, (dz, dy, high) in enumerate(CORNER):
            out_ref[n] = p_ref[H + own_layer(where, side, dz, nz), halo_row(dy, high, ny)]
    if first:
        c_low = where[C_TO] == 0
        for z in range(nz):
            at = nz * H + z * H // 8
            kc, kd = cr_ref[at, pl.ds(z * H % 8, H), :], dr_ref[at, pl.ds(z * H % 8, H), :]
            ke_ref[H + z, pl.ds(PAD, H), :] = jnp.where(c_low, kc, kd)
            ke_ref[H + z, pl.ds(PAD + H + ny, H), :] = jnp.where(c_low, kd, kc)
        for side, out_ref in enumerate((a_ref, b_ref)):
            for n, (dz, dy, high) in enumerate(CORNER):
                row = ke_ref[H + own_layer(where, side, dz, nz), pl.ds(PAD + halo_row(dy, high, ny), 1), :]
                out_ref[len(CORNER) + n // 8, pl.ds(n % 8, 1), :] = row


def fill_face(where, side, p_ref, ke_ref, face_ref, *, nz, ny):
    start = where[A_TO + side]

    def row(y, _):
        for z in range(H):
            p_ref[start + z, H + y] = face_ref[z * ny + y]
        return 0

    lax.fori_loop(0, ny, row, 0, unroll=4)
    if ke_ref is not None:
        for z in range(H):
            for g in range(ny // 8):
                ke_ref[start + z, pl.ds(PAD + H + 8 * g, 8), :] = face_ref[H * ny + z * (ny // 8) + g]


def fill_corner(where, side, p_ref, ke_ref, corner_ref, *, nz, ny):
    for n, (dz, dy, high) in enumerate(CORNER):
        p_ref[halo_layer(where, side, dz, nz), halo_row(dy, high, ny)] = corner_ref[n]
    if ke_ref is not None:
        for n, (dz, dy, high) in enumerate(CORNER):
            row = corner_ref[len(CORNER) + n // 8, pl.ds(n % 8, 1), :]
            ke_ref[halo_layer(where, side, dz, nz), pl.ds(PAD + halo_row(dy, high, ny), 1), :] = row


def coefficients(ke_ref, coef, z0, count, groups=None):
    diag_ref, wz_ref, wy_ref, wx_ref = coef
    deep, wide = diag_ref.shape[0], diag_ref.shape[1]
    lane = lanes()

    def one(i, _):
        z = z0 + i
        below, above = jnp.maximum(z - 1, 0), jnp.minimum(z + 1, deep - 1)
        for g in range(wide // 8) if groups is None else groups:
            at = PAD + 8 * g
            rows = pl.ds(8 * g, 8)
            k = ke_ref[z, pl.ds(at, 8), :]
            ku = ke_ref[above, pl.ds(at, 8), :]
            kn = ke_ref[z, pl.ds(at + 1, 8), :]
            around = (ke_ref[below, pl.ds(at, 8), :] + ku) + (ke_ref[z, pl.ds(at - 1, 8), :] + kn)
            inside = k > 0
            wz_ref[z, rows, :] = jnp.where(inside & (ku > 0), k + ku, 0.0)
            wy_ref[z, rows, :] = jnp.where(inside & (kn > 0), k + kn, 0.0)
            even, odd = halves(k)
            before = jnp.where(lane == 0, 0.0, pltpu.roll(odd, 1, 1))
            after = jnp.where(lane == 127, 0.0, pltpu.roll(even, 127, 1))
            even_around, odd_around = halves(around)
            shift = 2.0 * mid_point / half_width
            in_even, in_odd = even > 0, odd > 0
            diag_ref[z, rows, pl.ds(0, 128)] = jnp.where(in_even, 6.0 * even + (even_around + (before + odd)) - shift, 0.0)
            diag_ref[z, rows, pl.ds(128, 128)] = jnp.where(in_odd, 6.0 * odd + (odd_around + (even + after)) - shift, 0.0)
            wx_ref[z, rows, pl.ds(0, 128)] = jnp.where(in_even, even + odd, 0.0)
            wx_ref[z, rows, pl.ds(128, 128)] = jnp.where(in_odd & (lane < 127), odd + after, 0.0)
        return 0

    lax.fori_loop(0, count, one, 0)


def sweep(coef, now_ref, old_ref, store, z0, zcount, y0, ycount, first, group):
    diag_ref, wz_ref, wy_ref, wx_ref = coef
    both = (pl.ds(0, 128), pl.ds(128, 128))

    def rows(y, group):
        field = lambda z, y: [now_ref[z, y, :, part] for part in both]
        weight = lambda ref, z, y: halves(ref[z, pl.ds(y, 1), :])

        def across(value, weights):
            (even, odd), (inner, outer) = value, weights
            return inner * odd + pltpu.roll(outer * odd, 1, 1), inner * even + outer * pltpu.roll(even, 127, 1)

        below = [field(z0 - 1, y + r) for r in range(group)]
        here = [field(z0, y + r) for r in range(group)]
        wbelow = [weight(wz_ref, z0 - 1, y + r) for r in range(group)]
        for n in range(zcount):
            z = z0 + n
            above, wabove = [], []
            south, wsouth = field(z, y - 1), weight(wy_ref, z, y - 1)
            for r in range(group):
                north = here[r + 1] if r + 1 < group else field(z, y + group)
                above.append(field(z + 1, y + r))
                wabove.append(weight(wz_ref, z, y + r))
                wnorth, diag = weight(wy_ref, z, y + r), weight(diag_ref, z, y + r)
                sides = across(here[r], weight(wx_ref, z, y + r))
                for part in range(2):
                    pulled = wabove[r][part] * above[r][part] + wbelow[r][part] * below[r][part]
                    pulled += wnorth[part] * north[part] + wsouth[part] * south[part]
                    image = diag[part] * here[r][part] - (pulled + sides[part])
                    store(z, y + r, part, 0.5 * image if first else image - old_ref[z, y + r, :, both[part]])
                south, wsouth = here[r], wnorth
            below, here, wbelow = here, above, wabove

    def many(i, _):
        rows(y0 + group * i, group)
        return 0

    if ycount > group:
        lax.fori_loop(0, ycount // group, many, 0)
    else:
        rows(y0, ycount)
    if ycount > group and ycount % group:
        rows(y0 + ycount - ycount % group, ycount % group)


def steps(where, region, coef, p_ref, q_ref, last_store, *, nz, ny):
    def into(ref):
        def store(z, y, part, value):
            ref[z, y, :, pl.ds(128 * part, 128)] = value

        return store

    odd = where[Z_ODD] == 1
    for step in range(1, H + 1):
        h = H - step
        now, old = (p_ref, q_ref) if step % 2 == 1 else (q_ref, p_ref)
        store = last_store if step == H and last_store is not None else into(old)
        if region == "far":
            z0, zcount = jnp.where(odd, H + nz - step, H - h), h + step
        else:
            z0, zcount = jnp.where(odd, H - h, H + step), nz + h - step
        if region == "far":
            stretches = [(H - h, ny + 2 * h, FAR_ROWS[step - 1])]
        elif region == "inner":
            stretches = [(H + step, ny - 2 * step, INNER_ROWS[step - 1])]
        else:
            stretches = [(H - h, h + step, H), (H + ny - step, h + step, H)]
        for y0, ycount, group in stretches:
            sweep(coef, now, old, store, z0, zcount, y0, ycount, step == 1, group)


def near_layers(where):
    return jnp.where(where[Z_ODD] == 1, 0, H)


def inner_kernel(where, p_in, *rest, nz, ny, first):
    size = dict(nz=nz, ny=ny)
    if first:
        ke_in, face_ref, p_ref, ke_ref, q_ref, *coef = rest
        store = None
    else:
        *coef, face_ref, p_ref, q_ref, even_ref, odd_ref = rest
        ke_ref = None
        store = filtered_store((even_ref, odd_ref), **size)
    fill_face(where, 0, p_ref, ke_ref, face_ref, **size)
    if first:
        coefficients(ke_ref, coef, near_layers(where), nz + H)
    steps(where, "inner", coef, p_ref, q_ref, store, **size)


def edges_kernel(where, p_in, q_in, *rest, nz, ny, first):
    size = dict(nz=nz, ny=ny)
    if first:
        ke_in, *rest = rest
        corner_ref, p_ref, q_ref, ke_ref, *coef = rest[COEFS:]
        store = None
    else:
        *coef, corner_ref, even_in, odd_in, p_ref, q_ref, even_ref, odd_ref, g_ref = rest
        ke_ref = None
        store = filtered_store((even_ref, odd_ref), **size)
    fill_corner(where, 0, p_ref, ke_ref, corner_ref, **size)
    if first:
        coefficients(ke_ref, coef, near_layers(where), nz + H, groups=(0, (ny + 2 * H) // 8 - 1))
    steps(where, "edges", coef, p_ref, q_ref, store, **size)
    if not first:
        pairs = products((even_ref, odd_ref), where[A_FROM] * ny // 8, H * ny // 8, nz * ny, None)
        for n, total in enumerate(pairs):
            g_ref[n] = total


def far_kernel(where, p_in, q_in, *rest, nz, ny, first):
    size = dict(nz=nz, ny=ny)
    if first:
        ke_in, *rest = rest
        face_ref, corner_ref, p_ref, q_ref, ke_ref, *rest = rest[COEFS:]
        coef, faces = rest[:COEFS], rest[COEFS:]
        store = None
    else:
        *coef, face_ref, corner_ref, even_in, odd_in, pairs_ref, p_ref, q_ref, even_ref, odd_ref, g_ref = rest
        ke_ref = None
        store = filtered_store((even_ref, odd_ref), **size)
    fill_face(where, 1, p_ref, ke_ref, face_ref, **size)
    fill_corner(where, 1, p_ref, ke_ref, corner_ref, **size)
    if first:
        coefficients(ke_ref, coef, jnp.where(where[Z_ODD] == 1, H + nz - 1, 0), H + 1)
    steps(where, "far", coef, p_ref, q_ref, store, **size)
    if first:
        cut_faces(where, p_ref, faces, **size)
    else:
        sums = products((even_ref, odd_ref), where[B_FROM] * ny // 8, H * ny // 8, nz * ny, pairs_ref)
        row_of = lax.broadcasted_iota(jnp.int32, g_ref.shape, 0)
        col_of = lax.broadcasted_iota(jnp.int32, g_ref.shape, 1)
        gram = jnp.zeros(g_ref.shape, F32)
        for total, (v, w) in zip(sums, PAIRS):
            here = ((row_of == v) & (col_of == w)) | ((row_of == w) & (col_of == v))
            gram = jnp.where(here, jnp.sum(total), gram)
        g_ref[...] = gram


PAIRS = [(v, w) for v in range(8) for w in range(v + 1)]


def filtered_store(outs, *, nz, ny):
    def store(z, y, part, value):
        outs[part][pl.ds((z - H) * ny + (y - H), 8, stride=nz * ny), :] = value

    return store


def products(parts, start, count, cells, initial):
    def group(i, sums):
        out = list(sums)
        for ref in parts:
            rows = [ref[pl.ds(pl.multiple_of(v * cells + (start + i) * 8, 8), 8), :] for v in range(8)]
            for n, (v, w) in enumerate(PAIRS):
                out[n] = out[n] + rows[v] * rows[w]
        return tuple(out)

    zero = [jnp.zeros((8, 128), F32) if initial is None else initial[n] for n in range(len(PAIRS))]
    return lax.fori_loop(0, count, group, tuple(zero))


def basis_kernel(g_ref, even_ref, odd_ref, out_ref, made_ref, ready_ref, sems, *, scale, blocks):
    vectors, cells = made_ref.shape[0], made_ref.shape[1]
    row = lax.broadcasted_iota(jnp.int32, (vectors, 128), 0)
    col = lax.broadcasted_iota(jnp.int32, (vectors, 128), 1)
    gram = jnp.sum(g_ref[...], axis=0)
    both = jnp.where(col < vectors, gram, jnp.where(col - vectors == row, 1.0, 0.0))
    scales = jnp.zeros((vectors, 128), F32)
    for k in range(vectors):
        pivot_row = jnp.broadcast_to(both[k : k + 1, :], both.shape)
        pivot = jnp.broadcast_to(pivot_row[:, k : k + 1], both.shape)
        scales = jnp.where(row == k, scale * lax.rsqrt(pivot), scales)
        if k + 1 < vectors:
            factor = jnp.broadcast_to(both[:, k : k + 1], both.shape) / pivot
            both = both - jnp.where(row > k, factor, 0.0) * pivot_row
    both = both * scales
    spread = lambda v, w: jnp.broadcast_to(both[v : v + 1, vectors + w : vectors + w + 1], (8, 128))
    weights = [[spread(v, w) for w in range(v + 1)] for v in range(vectors)]
    matrix = even_first(back=True)
    count = cells // blocks
    copies = []
    for block in range(blocks):
        first = block * count

        def combine(i, _, first=first):
            at = pl.ds(pl.multiple_of(first + i * 8, 8), 8)
            for part, ref in enumerate((even_ref, odd_ref)):
                field = [ref[v, at, :] for v in range(vectors)]
                for v in range(vectors):
                    total = weights[v][0] * field[0]
                    for w in range(1, v + 1):
                        total = total + weights[v][w] * field[w]
                    made_ref[v, at, pl.ds(part * 128, 128)] = total
            return 0

        lax.fori_loop(0, count // 8, combine, 0, unroll=2)
        rows = pl.ds(first, count)
        made = permuted(made_ref[:, rows, :].reshape(vectors * count, 256), matrix, terms=2)
        ready_ref[:, rows, :] = made.reshape(vectors, count, 256)
        copies.append(pltpu.make_async_copy(ready_ref.at[:, rows, :], out_ref.at[:, rows, :], sems.at[block]))
        copies[-1].start()
    for copy in copies:
        copy.wait()


def basis(gram, even, odd, cells, scale):
    vectors = gram.shape[1]
    blocks = 2
    shape = (vectors, cells, 256)
    return pl.pallas_call(
        functools.partial(basis_kernel, scale=scale, blocks=blocks),
        out_shape=jax.ShapeDtypeStruct(shape, F32),
        in_specs=[pl.BlockSpec(memory_space=pltpu.VMEM)] * 3,
        out_specs=pl.BlockSpec(memory_space=pltpu.HBM),
        scratch_shapes=[pltpu.VMEM(shape, F32), pltpu.VMEM(shape, F32), pltpu.SemaphoreType.DMA((blocks,))],
        compiler_params=pltpu.CompilerParams(vmem_limit_bytes=16 << 20),
        name="basis",
    )(gram, even.reshape(vectors, cells, 128), odd.reshape(vectors, cells, 128))


def shards(block, conduct):
    vectors, nz, ny, nx = block.shape
    zcount, ycount = lax.axis_size("gz"), lax.axis_size("gy")
    zi, yi = lax.axis_index("gz"), lax.axis_index("gy")
    a_pairs = ("gz", [(i, i ^ 1) for i in range(zcount)])
    b_pairs = ("gz", [(i, ((i + 1) ^ 1) - 1) for i in range(1, zcount - 1)])
    c_pairs = ("gy", [(i, i ^ 1) for i in range(ycount)])
    d_pairs = ("gy", [(i, ((i + 1) ^ 1) - 1) for i in range(1, ycount - 1)])
    zodd, yodd = zi % 2, yi % 2
    where = jnp.stack([
        (1 - yodd) * (ny - H), yodd * (ny - H), (1 - zodd) * (nz - H), zodd * (nz - H),
        (1 - yodd) * (ny + H), yodd * (ny + H), (1 - zodd) * (nz + H), zodd * (nz + H), zodd,
    ]).astype(jnp.int32)
    wide, deep = ny + 2 * H, nz + 2 * H
    row = (vectors, nx)
    cells = nz * ny
    field, ke, weights = (deep, wide, *row), (deep, wide + 2 * PAD, nx), [(deep, wide, nx)] * COEFS
    halves_shape = [(vectors * cells, nx // 2)] * 2
    corner = len(CORNER)
    kernel = lambda f, **more: functools.partial(f, nz=nz, ny=ny, **more)
    swap = lambda payload, pairs: lax.ppermute(payload, *pairs)

    def begin(a, b, c, d):
        c = swap(c, c_pairs)
        d = swap(d, d_pairs)
        a = swap(a, a_pairs)
        b = swap(b, b_pairs)
        return a, b, c, d

    def corners(p, ke, c, d):
        first = ke is not None
        n = corner + 2 if first else corner
        keep = [field] + ([ke.shape] if first else [])
        args = (where, p) + ((ke,) if first else ()) + (c, d)
        alias = {1: 0, 2: 1} if first else {1: 0}
        *kept, ac, bc = call(kernel(corner_kernel, first=first), keep + [(n, *row)] * 2, args, alias)
        ac = swap(ac, a_pairs)
        bc = swap(bc, b_pairs)
        return kept, ac, bc

    inner_flops, edge_flops, far_flops = 16_000_000, 4_000_000, 12_000_000
    extra_z, extra_y = H * ny // 8, nz * H // 8
    p, k, a, b, c, d = call(
        kernel(turn_kernel),
        [field, ke, (H * ny + extra_z, *row), (H * ny + extra_z, *row), (nz * H + extra_y, *row), (nz * H + extra_y, *row)],
        (where, *(pltpu.with_memory_space_constraint(arg, pltpu.HBM) for arg in (block, conduct))), space=pltpu.HBM,
        scratch=[pltpu.VMEM(conduct.shape, F32), pltpu.SemaphoreType.DMA((vectors,)), pltpu.SemaphoreType.DMA])
    a, b, c, d = begin(a, b, c, d)
    p, k, q, *coef = call(kernel(inner_kernel, first=True), [field, ke, field, *weights], (where, p, k, a),
                          {1: 0, 2: 1}, flops=inner_flops)
    (p, k), ac, bc = corners(p, k, c, d)
    p, q, k, *coef = call(
        kernel(edges_kernel, first=True), [field, field, ke, *weights], (where, p, q, k, *coef, ac),
        {n + 1: n for n in range(3 + COEFS)}, flops=edge_flops)
    p, q, k, *rest = call(
        kernel(far_kernel, first=True),
        [field, field, ke, *weights, (H * ny, *row), (H * ny, *row), (nz * H, *row), (nz * H, *row)],
        (where, p, q, k, *coef, b, bc), {n + 1: n for n in range(3 + COEFS)}, flops=far_flops)
    coef, (a, b, c, d) = rest[:COEFS], rest[COEFS:]
    a, b, c, d = begin(a, b, c, d)
    p, q, left, right = call(kernel(inner_kernel, first=False), [field, field, *halves_shape], (where, p, *coef, a),
                             {1: 0}, flops=inner_flops)
    (p,), ac, bc = corners(p, None, c, d)
    p, q, left, right, pairs = call(
        kernel(edges_kernel, first=False), [field, field, *halves_shape, (len(PAIRS), 8, 128)],
        (where, p, q, *coef, ac, left, right), {1: 0, 2: 1, COEFS + 4: 2, COEFS + 5: 3},
        flops=edge_flops)
    _, _, left, right, gram = call(
        kernel(far_kernel, first=False), [field, field, *halves_shape, (vectors, 128)],
        (where, p, q, *coef, b, bc, left, right, pairs), {1: 0, 2: 1, COEFS + 5: 2, COEFS + 6: 3},
        flops=far_flops)
    gram = sum_everywhere(gram, zcount, ycount)
    out = basis(gram, left, right, cells, math.sqrt(nx * cells * zcount * ycount))
    return out.reshape(block.shape)


def sum_everywhere(part, zcount, ycount):
    part = part + lax.ppermute(part, "gz", [(i, i ^ 1) for i in range(zcount)])
    line = 8
    planes = zcount // (2 * line)

    def flat(y, x, z, core):
        return ((y * line + z) * 2 + core) * ycount + x

    planar = [[flat(y, x, z, core) for y in range(planes) for x in range(ycount)] for z in range(line) for core in range(2)]
    part = jnp.sum(gathered(part, ("gz", "gy"), planar), axis=0)
    lines = [[(y * line + z) * 2 + core for z in range(line)] for y in range(planes) for core in range(2)]
    return gathered(part, "gz", lines)


def gathered(part, axes, groups):
    n = len(groups[0])
    copies = jnp.broadcast_to(part[None], (n, *part.shape))
    return lax.all_to_all(copies, axes, 0, 0, axis_index_groups=groups, tiled=True)


def solution(mesh):
    in_specs = (P(None, "gz", "gy", None), P("gz", "gy", None))
    out_specs = P(None, "gz", "gy", None)
    return jax.shard_map(shards, mesh=mesh, in_specs=in_specs, out_specs=out_specs, check_vma=False)
```

```python
import functools
import math

import jax
import jax.numpy as jnp
from jax import lax
from jax.experimental import pallas as pl
from jax.experimental.pallas import tpu as pltpu
from jax.sharding import PartitionSpec as P


mid_point = 12.75
half_width = 11.25
F32 = jnp.float32
H = 4
COEFS = 4
CHUNK = 4
INNER_ROWS = (6, 7, 13, 12)
FAR_ROWS = (19, 12, 17, 16)
PAD = 8

C_FROM, D_FROM, A_FROM, B_FROM = range(4)
C_TO, D_TO, A_TO, _ = range(4, 8)
Z_ODD = 8

CORNER = [(dz, dy, high) for dz in range(1, H) for dy in range(1, H - dz + 1) for high in (0, 1)]


def call(kernel, outs, args, alias=None, scratch=(), flops=0, limit=16 << 20, space=pltpu.VMEM):
    specs = [pl.BlockSpec(memory_space=pltpu.SMEM)]
    specs += [pl.BlockSpec(memory_space=space)] * (len(args) - 1)
    return pl.pallas_call(
        kernel,
        out_shape=[jax.ShapeDtypeStruct(s, F32) for s in outs],
        in_specs=specs,
        out_specs=[pl.BlockSpec(memory_space=pltpu.VMEM)] * len(outs),
        scratch_shapes=list(scratch),
        input_output_aliases=alias or {},
        compiler_params=pltpu.CompilerParams(vmem_limit_bytes=limit),
        cost_estimate=pl.CostEstimate(flops=flops, bytes_accessed=1 << 16, transcendentals=0),
    )(*args)


def halves(value):
    width = value.shape[-1] // 2
    return value[..., :width], value[..., width:]


def lanes():
    return lax.broadcasted_iota(jnp.int32, (8, 128), 1)


def even_first(back=False):
    row, col = (lax.broadcasted_iota(jnp.int32, (256, 256), axis) for axis in ((1, 0) if back else (0, 1)))
    return jnp.where(row == 2 * (col % 128) + col // 128, 1.0, 0.0).astype(jnp.bfloat16)


def permuted(value, matrix, terms=3):
    total = None
    for term in range(terms):
        high = value.astype(jnp.bfloat16)
        moved = jnp.dot(high, matrix, preferred_element_type=F32)
        total = moved if total is None else total + moved
        if term + 1 < terms:
            value = value - high.astype(F32)
    return total


def cut_layers(start, p_ref, out_ref, *, ny):
    def row(y, _):
        for z in range(H):
            out_ref[z * ny + y] = p_ref[H + start + z, H + y]
        return 0

    lax.fori_loop(0, ny, row, 0, unroll=4)


def cut_rows(start, p_ref, out_ref, *, nz):
    def layer(z, _):
        for j in range(H):
            out_ref[z * H + j] = p_ref[H + z, H + start + j]
        return 0

    lax.fori_loop(0, nz, layer, 0, unroll=4)


def turn_kernel(where, x_ref, k_ref, p_ref, ke_ref, *rest, nz, ny):
    faces, coef, (k_here, sems, k_sem) = rest[:4], rest[4 : 4 + COEFS], rest[4 + COEFS :]
    a_ref, b_ref, c_ref, d_ref = faces
    vectors = p_ref.shape[2]
    k_copy = pltpu.make_async_copy(k_ref, k_here, k_sem)
    copies = [
        pltpu.make_async_copy(x_ref.at[v], p_ref.at[pl.ds(H, nz), pl.ds(H, ny), v, :], sems.at[v]) for v in range(vectors)
    ]
    k_copy.start()
    for copy in copies:
        copy.start()
    k_copy.wait()
    matrix = even_first()
    nx = p_ref.shape[3]
    k_turned = permuted(k_here[...].reshape(nz * ny, nx) * (1.0 / half_width), matrix)
    for z in range(nz):
        ke_ref[H + z, pl.ds(PAD + H, ny), :] = k_turned[z * ny : (z + 1) * ny]
    coefficients(ke_ref, coef, H, nz)
    for copy in copies:
        copy.wait()
    for z in range(0, nz, CHUNK):
        block = p_ref.at[pl.ds(H + z, CHUNK), pl.ds(H, ny)]
        block[...] = permuted(block[...].reshape(CHUNK * ny * vectors, nx), matrix).reshape(CHUNK, ny, vectors, nx)
    cut_layers(where[A_FROM], p_ref, a_ref, ny=ny)
    cut_layers(where[B_FROM], p_ref, b_ref, ny=ny)
    cut_rows(where[C_FROM], p_ref, c_ref, nz=nz)
    cut_rows(where[D_FROM], p_ref, d_ref, nz=nz)
    c_low = where[C_FROM] == 0
    for z in range(nz):
        low, high = ke_ref[H + z, pl.ds(PAD + H, H), :], ke_ref[H + z, pl.ds(PAD + ny, H), :]
        at = nz * H + z * H // 8
        c_ref[at, pl.ds(z * H % 8, H), :] = jnp.where(c_low, low, high)
        d_ref[at, pl.ds(z * H % 8, H), :] = jnp.where(c_low, high, low)
    for z in range(H):
        for g in range(ny // 8):
            for out_ref, start in ((a_ref, where[A_FROM]), (b_ref, where[B_FROM])):
                out_ref[H * ny + z * (ny // 8) + g] = ke_ref[H + start + z, pl.ds(PAD + H + 8 * g, 8), :]


def own_layer(where, side, dz, nz):
    low = where[Z_ODD] == 1 - side
    return jnp.where(low, dz - 1, nz - dz)


def halo_layer(where, side, dz, nz):
    low = where[Z_ODD] == 1 - side
    return jnp.where(low, H - dz, H + nz + dz - 1)


def halo_row(dy, high, ny):
    return H + ny + dy - 1 if high else H - dy


def corner_kernel(where, p_in, *rest, nz, ny, first):
    if first:
        _, cr_ref, dr_ref, p_ref, ke_ref, a_ref, b_ref = rest
    else:
        cr_ref, dr_ref, p_ref, a_ref, b_ref = rest

    def layer(z, _):
        for j in range(H):
            p_ref[H + z, where[C_TO] + j] = cr_ref[z * H + j]
            p_ref[H + z, where[D_TO] + j] = dr_ref[z * H + j]
        return 0

    lax.fori_loop(0, nz, layer, 0, unroll=2)
    for side, out_ref in enumerate((a_ref, b_ref)):
        for n, (dz, dy, high) in enumerate(CORNER):
            out_ref[n] = p_ref[H + own_layer(where, side, dz, nz), halo_row(dy, high, ny)]
    if first:
        c_low = where[C_TO] == 0
        for z in range(nz):
            at = nz * H + z * H // 8
            kc, kd = cr_ref[at, pl.ds(z * H % 8, H), :], dr_ref[at, pl.ds(z * H % 8, H), :]
            ke_ref[H + z, pl.ds(PAD, H), :] = jnp.where(c_low, kc, kd)
            ke_ref[H + z, pl.ds(PAD + H + ny, H), :] = jnp.where(c_low, kd, kc)
        for side, out_ref in enumerate((a_ref, b_ref)):
            for n, (dz, dy, high) in enumerate(CORNER):
                row = ke_ref[H + own_layer(where, side, dz, nz), pl.ds(PAD + halo_row(dy, high, ny), 1), :]
                out_ref[len(CORNER) + n // 8, pl.ds(n % 8, 1), :] = row


def fill_face(where, side, p_ref, ke_ref, face_ref, *, nz, ny):
    start = where[A_TO + side]

    def row(y, _):
        for z in range(H):
            p_ref[start + z, H + y] = face_ref[z * ny + y]
        return 0

    lax.fori_loop(0, ny, row, 0, unroll=4)
    if ke_ref is not None:
        for z in range(H):
            for g in range(ny // 8):
                ke_ref[start + z, pl.ds(PAD + H + 8 * g, 8), :] = face_ref[H * ny + z * (ny // 8) + g]


def fill_corner(where, side, p_ref, ke_ref, corner_ref, *, nz, ny):
    for n, (dz, dy, high) in enumerate(CORNER):
        p_ref[halo_layer(where, side, dz, nz), halo_row(dy, high, ny)] = corner_ref[n]
    if ke_ref is not None:
        for n, (dz, dy, high) in enumerate(CORNER):
            row = corner_ref[len(CORNER) + n // 8, pl.ds(n % 8, 1), :]
            ke_ref[halo_layer(where, side, dz, nz), pl.ds(PAD + halo_row(dy, high, ny), 1), :] = row


def coefficients(ke_ref, coef, z0, count, groups=None):
    diag_ref, wz_ref, wy_ref, wx_ref = coef
    deep, wide = diag_ref.shape[0], diag_ref.shape[1]
    lane = lanes()

    def one(i, _):
        z = z0 + i
        below, above = jnp.maximum(z - 1, 0), jnp.minimum(z + 1, deep - 1)
        for g in range(wide // 8) if groups is None else groups:
            at = PAD + 8 * g
            rows = pl.ds(8 * g, 8)
            k = ke_ref[z, pl.ds(at, 8), :]
            ku = ke_ref[above, pl.ds(at, 8), :]
            kn = ke_ref[z, pl.ds(at + 1, 8), :]
            around = (ke_ref[below, pl.ds(at, 8), :] + ku) + (ke_ref[z, pl.ds(at - 1, 8), :] + kn)
            inside = k > 0
            wz_ref[z, rows, :] = jnp.where(inside & (ku > 0), k + ku, 0.0)
            wy_ref[z, rows, :] = jnp.where(inside & (kn > 0), k + kn, 0.0)
            even, odd = halves(k)
            before = jnp.where(lane == 0, 0.0, pltpu.roll(odd, 1, 1))
            after = jnp.where(lane == 127, 0.0, pltpu.roll(even, 127, 1))
            even_around, odd_around = halves(around)
            shift = 2.0 * mid_point / half_width
            in_even, in_odd = even > 0, odd > 0
            diag_ref[z, rows, pl.ds(0, 128)] = jnp.where(in_even, 6.0 * even + (even_around + (before + odd)) - shift, 0.0)
            diag_ref[z, rows, pl.ds(128, 128)] = jnp.where(in_odd, 6.0 * odd + (odd_around + (even + after)) - shift, 0.0)
            wx_ref[z, rows, pl.ds(0, 128)] = jnp.where(in_even, even + odd, 0.0)
            wx_ref[z, rows, pl.ds(128, 128)] = jnp.where(in_odd & (lane < 127), odd + after, 0.0)
        return 0

    lax.fori_loop(0, count, one, 0)


def sweep(coef, now_ref, old_ref, store, z0, zcount, y0, ycount, first, group):
    diag_ref, wz_ref, wy_ref, wx_ref = coef
    both = (pl.ds(0, 128), pl.ds(128, 128))

    def rows(y, group):
        field = lambda z, y: [now_ref[z, y, :, part] for part in both]
        weight = lambda ref, z, y: halves(ref[z, pl.ds(y, 1), :])

        def across(value, weights):
            (even, odd), (inner, outer) = value, weights
            return inner * odd + pltpu.roll(outer * odd, 1, 1), inner * even + outer * pltpu.roll(even, 127, 1)

        below = [field(z0 - 1, y + r) for r in range(group)]
        here = [field(z0, y + r) for r in range(group)]
        wbelow = [weight(wz_ref, z0 - 1, y + r) for r in range(group)]
        for n in range(zcount):
            z = z0 + n
            above, wabove = [], []
            south, wsouth = field(z, y - 1), weight(wy_ref, z, y - 1)
            for r in range(group):
                north = here[r + 1] if r + 1 < group else field(z, y + group)
                above.append(field(z + 1, y + r))
                wabove.append(weight(wz_ref, z, y + r))
                wnorth, diag = weight(wy_ref, z, y + r), weight(diag_ref, z, y + r)
                sides = across(here[r], weight(wx_ref, z, y + r))
                for part in range(2):
                    pulled = wabove[r][part] * above[r][part] + wbelow[r][part] * below[r][part]
                    pulled += wnorth[part] * north[part] + wsouth[part] * south[part]
                    image = diag[part] * here[r][part] - (pulled + sides[part])
                    store(z, y + r, part, 0.5 * image if first else image - old_ref[z, y + r, :, both[part]])
                south, wsouth = here[r], wnorth
            below, here, wbelow = here, above, wabove

    def many(i, _):
        rows(y0 + group * i, group)
        return 0

    if ycount > group:
        lax.fori_loop(0, ycount // group, many, 0)
    else:
        rows(y0, ycount)
    if ycount > group and ycount % group:
        rows(y0 + ycount - ycount % group, ycount % group)


def steps(where, region, coef, p_ref, q_ref, last_store, *, nz, ny):
    def into(ref):
        def store(z, y, part, value):
            ref[z, y, :, pl.ds(128 * part, 128)] = value

        return store

    odd = where[Z_ODD] == 1
    for step in range(1, H + 1):
        h = H - step
        now, old = (p_ref, q_ref) if step % 2 == 1 else (q_ref, p_ref)
        store = last_store if step == H and last_store is not None else into(old)
        if region == "far":
            z0, zcount = jnp.where(odd, H + nz - step, H - h), h + step
        else:
            z0, zcount = jnp.where(odd, H - h, H + step), nz + h - step
        if region == "far":
            stretches = [(H - h, ny + 2 * h, FAR_ROWS[step - 1])]
        elif region == "inner":
            stretches = [(H + step, ny - 2 * step, INNER_ROWS[step - 1])]
        else:
            stretches = [(H - h, h + step, H), (H + ny - step, h + step, H)]
        for y0, ycount, group in stretches:
            sweep(coef, now, old, store, z0, zcount, y0, ycount, step == 1, group)


def near_layers(where):
    return jnp.where(where[Z_ODD] == 1, 0, H)


def inner_kernel(where, p_in, *rest, nz, ny, first):
    size = dict(nz=nz, ny=ny)
    if first:
        ke_in, *rest = rest
        face_ref, p_ref, ke_ref, q_ref, *coef = rest[COEFS:]
        store = None
    else:
        *coef, face_ref, p_ref, q_ref, even_ref, odd_ref = rest
        ke_ref = None
        store = filtered_store((even_ref, odd_ref), **size)
    fill_face(where, 0, p_ref, ke_ref, face_ref, **size)
    if first:
        coefficients(ke_ref, coef, jnp.where(where[Z_ODD] == 1, 0, H + nz - 1), H + 1)
    steps(where, "inner", coef, p_ref, q_ref, store, **size)


def edges_kernel(where, p_in, q_in, *rest, nz, ny, first):
    size = dict(nz=nz, ny=ny)
    if first:
        ke_in, *rest = rest
        corner_ref, p_ref, q_ref, ke_ref, *rest = rest[COEFS:]
        coef, out_ref = rest[:COEFS], rest[COEFS]
        store = None
    else:
        *coef, corner_ref, even_in, odd_in, p_ref, q_ref, even_ref, odd_ref, g_ref = rest
        ke_ref = None
        store = filtered_store((even_ref, odd_ref), **size)
    fill_corner(where, 0, p_ref, ke_ref, corner_ref, **size)
    if first:
        coefficients(ke_ref, coef, near_layers(where), nz + H, groups=(0, (ny + 2 * H) // 8 - 1))
    steps(where, "edges", coef, p_ref, q_ref, store, **size)
    if first:
        cut_layers(where[A_FROM], p_ref, out_ref, ny=ny)
    else:
        pairs = products((even_ref, odd_ref), where[A_FROM] * ny // 8, H * ny // 8, nz * ny, None)
        for n, total in enumerate(pairs):
            g_ref[n] = total


def far_kernel(where, p_in, q_in, *rest, nz, ny, first):
    size = dict(nz=nz, ny=ny)
    if first:
        ke_in, *rest = rest
        face_ref, corner_ref, p_ref, q_ref, ke_ref, *rest = rest[COEFS:]
        coef, faces = rest[:COEFS], rest[COEFS:]
        store = None
    else:
        *coef, face_ref, corner_ref, even_in, odd_in, pairs_ref, p_ref, q_ref, even_ref, odd_ref, g_ref = rest
        ke_ref = None
        store = filtered_store((even_ref, odd_ref), **size)
    fill_face(where, 1, p_ref, ke_ref, face_ref, **size)
    fill_corner(where, 1, p_ref, ke_ref, corner_ref, **size)
    if first:
        coefficients(ke_ref, coef, jnp.where(where[Z_ODD] == 1, H + nz - 1, 0), H + 1)
    steps(where, "far", coef, p_ref, q_ref, store, **size)
    if first:
        b_ref, c_ref, d_ref = faces
        cut_layers(where[B_FROM], p_ref, b_ref, ny=ny)
        cut_rows(where[C_FROM], p_ref, c_ref, nz=nz)
        cut_rows(where[D_FROM], p_ref, d_ref, nz=nz)
    else:
        sums = products((even_ref, odd_ref), where[B_FROM] * ny // 8, H * ny // 8, nz * ny, pairs_ref)
        row_of = lax.broadcasted_iota(jnp.int32, g_ref.shape, 0)
        col_of = lax.broadcasted_iota(jnp.int32, g_ref.shape, 1)
        gram = jnp.zeros(g_ref.shape, F32)
        for total, (v, w) in zip(sums, PAIRS):
            here = ((row_of == v) & (col_of == w)) | ((row_of == w) & (col_of == v))
            gram = jnp.where(here, jnp.sum(total), gram)
        g_ref[...] = gram


PAIRS = [(v, w) for v in range(8) for w in range(v + 1)]


def filtered_store(outs, *, nz, ny):
    def store(z, y, part, value):
        outs[part][pl.ds((z - H) * ny + (y - H), 8, stride=nz * ny), :] = value

    return store


def products(parts, start, count, cells, initial):
    def group(i, sums):
        out = list(sums)
        for ref in parts:
            rows = [ref[pl.ds(pl.multiple_of(v * cells + (start + i) * 8, 8), 8), :] for v in range(8)]
            for n, (v, w) in enumerate(PAIRS):
                out[n] = out[n] + rows[v] * rows[w]
        return tuple(out)

    zero = [jnp.zeros((8, 128), F32) if initial is None else initial[n] for n in range(len(PAIRS))]
    return lax.fori_loop(0, count, group, tuple(zero))


def basis_kernel(g_ref, even_ref, odd_ref, out_ref, made_ref, ready_ref, sems, *, scale, blocks):
    vectors, cells = made_ref.shape[0], made_ref.shape[1]
    row = lax.broadcasted_iota(jnp.int32, (vectors, 128), 0)
    col = lax.broadcasted_iota(jnp.int32, (vectors, 128), 1)
    gram = jnp.sum(g_ref[...], axis=0)
    both = jnp.where(col < vectors, gram, jnp.where(col - vectors == row, 1.0, 0.0))
    scales = jnp.zeros((vectors, 128), F32)
    for k in range(vectors):
        pivot_row = jnp.broadcast_to(both[k : k + 1, :], both.shape)
        pivot = jnp.broadcast_to(pivot_row[:, k : k + 1], both.shape)
        scales = jnp.where(row == k, scale * lax.rsqrt(pivot), scales)
        if k + 1 < vectors:
            factor = jnp.broadcast_to(both[:, k : k + 1], both.shape) / pivot
            both = both - jnp.where(row > k, factor, 0.0) * pivot_row
    both = both * scales
    spread = lambda v, w: jnp.broadcast_to(both[v : v + 1, vectors + w : vectors + w + 1], (8, 128))
    weights = [[spread(v, w) for w in range(v + 1)] for v in range(vectors)]
    matrix = even_first(back=True)
    count = cells // blocks
    copies = []
    for block in range(blocks):
        first = block * count

        def combine(i, _, first=first):
            at = pl.ds(pl.multiple_of(first + i * 8, 8), 8)
            for part, ref in enumerate((even_ref, odd_ref)):
                field = [ref[v, at, :] for v in range(vectors)]
                for v in range(vectors):
                    total = weights[v][0] * field[0]
                    for w in range(1, v + 1):
                        total = total + weights[v][w] * field[w]
                    made_ref[v, at, pl.ds(part * 128, 128)] = total
            return 0

        lax.fori_loop(0, count // 8, combine, 0, unroll=2)
        rows = pl.ds(first, count)
        made = permuted(made_ref[:, rows, :].reshape(vectors * count, 256), matrix, terms=2)
        ready_ref[:, rows, :] = made.reshape(vectors, count, 256)
        copies.append(pltpu.make_async_copy(ready_ref.at[:, rows, :], out_ref.at[:, rows, :], sems.at[block]))
        copies[-1].start()
    for copy in copies:
        copy.wait()


def basis(gram, even, odd, cells, scale):
    vectors = gram.shape[1]
    blocks = 2
    shape = (vectors, cells, 256)
    return pl.pallas_call(
        functools.partial(basis_kernel, scale=scale, blocks=blocks),
        out_shape=jax.ShapeDtypeStruct(shape, F32),
        in_specs=[pl.BlockSpec(memory_space=pltpu.VMEM)] * 3,
        out_specs=pl.BlockSpec(memory_space=pltpu.HBM),
        scratch_shapes=[pltpu.VMEM(shape, F32), pltpu.VMEM(shape, F32), pltpu.SemaphoreType.DMA((blocks,))],
        compiler_params=pltpu.CompilerParams(vmem_limit_bytes=16 << 20),
        name="basis",
    )(gram, even.reshape(vectors, cells, 128), odd.reshape(vectors, cells, 128))


def shards(block, conduct):
    vectors, nz, ny, nx = block.shape
    zcount, ycount = lax.axis_size("gz"), lax.axis_size("gy")
    zi, yi = lax.axis_index("gz"), lax.axis_index("gy")
    a_pairs = ("gz", [(i, i ^ 1) for i in range(zcount)])
    b_pairs = ("gz", [(i, ((i + 1) ^ 1) - 1) for i in range(1, zcount - 1)])
    c_pairs = ("gy", [(i, i ^ 1) for i in range(ycount)])
    d_pairs = ("gy", [(i, ((i + 1) ^ 1) - 1) for i in range(1, ycount - 1)])
    zodd, yodd = zi % 2, yi % 2
    where = jnp.stack([
        (1 - yodd) * (ny - H), yodd * (ny - H), (1 - zodd) * (nz - H), zodd * (nz - H),
        (1 - yodd) * (ny + H), yodd * (ny + H), (1 - zodd) * (nz + H), zodd * (nz + H), zodd,
    ]).astype(jnp.int32)
    wide, deep = ny + 2 * H, nz + 2 * H
    row = (vectors, nx)
    cells = nz * ny
    field, ke, weights = (deep, wide, *row), (deep, wide + 2 * PAD, nx), [(deep, wide, nx)] * COEFS
    halves_shape = [(vectors * cells, nx // 2)] * 2
    corner = len(CORNER)
    kernel = lambda f, **more: functools.partial(f, nz=nz, ny=ny, **more)
    swap = lambda payload, pairs: lax.ppermute(payload, *pairs)

    def begin(b, c, d):
        c = swap(c, c_pairs)
        d = swap(d, d_pairs)
        b = swap(b, b_pairs)
        return b, c, d

    def corners(p, ke, c, d):
        first = ke is not None
        n = corner + 2 if first else corner
        keep = [field] + ([ke.shape] if first else [])
        args = (where, p) + ((ke,) if first else ()) + (c, d)
        alias = {1: 0, 2: 1} if first else {1: 0}
        *kept, ac, bc = call(kernel(corner_kernel, first=first), keep + [(n, *row)] * 2, args, alias)
        ac = swap(ac, a_pairs)
        bc = swap(bc, b_pairs)
        return kept, ac, bc

    inner_flops, edge_flops, far_flops = 16_000_000, 4_000_000, 12_000_000
    extra_z, extra_y = H * ny // 8, nz * H // 8
    p, k, a, b, c, d, *coef = call(
        kernel(turn_kernel),
        [field, ke, (H * ny + extra_z, *row), (H * ny + extra_z, *row), (nz * H + extra_y, *row), (nz * H + extra_y, *row), *weights],
        (where, *(pltpu.with_memory_space_constraint(arg, pltpu.HBM) for arg in (block, conduct))), space=pltpu.HBM,
        scratch=[pltpu.VMEM(conduct.shape, F32), pltpu.SemaphoreType.DMA((vectors,)), pltpu.SemaphoreType.DMA])
    b, c, d = begin(b, c, d)
    a = swap(a, a_pairs)
    p, k, q, *coef = call(kernel(inner_kernel, first=True), [field, ke, field, *weights], (where, p, k, *coef, a),
                          {1: 0, 2: 1, **{3 + n: 3 + n for n in range(COEFS)}}, flops=inner_flops)
    (p, k), ac, bc = corners(p, k, c, d)
    p, q, k, *coef, a = call(
        kernel(edges_kernel, first=True), [field, field, ke, *weights, (H * ny, *row)], (where, p, q, k, *coef, ac),
        {n + 1: n for n in range(3 + COEFS)}, flops=edge_flops)
    a = swap(a, a_pairs)
    p, q, k, *rest = call(
        kernel(far_kernel, first=True),
        [field, field, ke, *weights, (H * ny, *row), (nz * H, *row), (nz * H, *row)],
        (where, p, q, k, *coef, b, bc), {n + 1: n for n in range(3 + COEFS)}, flops=far_flops)
    coef, (b, c, d) = rest[:COEFS], rest[COEFS:]
    b, c, d = begin(b, c, d)
    p, q, left, right = call(kernel(inner_kernel, first=False), [field, field, *halves_shape], (where, p, *coef, a),
                             {1: 0}, flops=inner_flops)
    (p,), ac, bc = corners(p, None, c, d)
    p, q, left, right, pairs = call(
        kernel(edges_kernel, first=False), [field, field, *halves_shape, (len(PAIRS), 8, 128)],
        (where, p, q, *coef, ac, left, right), {1: 0, 2: 1, COEFS + 4: 2, COEFS + 5: 3},
        flops=edge_flops)
    _, _, left, right, gram = call(
        kernel(far_kernel, first=False), [field, field, *halves_shape, (vectors, 128)],
        (where, p, q, *coef, b, bc, left, right, pairs), {1: 0, 2: 1, COEFS + 5: 2, COEFS + 6: 3},
        flops=far_flops)
    gram = sum_everywhere(gram, zcount, ycount)
    out = basis(gram, left, right, cells, math.sqrt(nx * cells * zcount * ycount))
    return out.reshape(block.shape)


def sum_everywhere(part, zcount, ycount):
    part = part + lax.ppermute(part, "gz", [(i, i ^ 1) for i in range(zcount)])
    line = 8
    planes = zcount // (2 * line)

    def flat(y, x, z, core):
        return ((y * line + z) * 2 + core) * ycount + x

    planar = [[flat(y, x, z, core) for y in range(planes) for x in range(ycount)] for z in range(line) for core in range(2)]
    lines = [[(y * line + z) * 2 + core for z in range(line)] for y in range(planes) for core in range(2)]
    part = jnp.sum(gathered(part, "gz", lines), axis=0)
    return gathered(part, ("gz", "gy"), planar)


def gathered(part, axes, groups):
    n = len(groups[0])
    copies = jnp.broadcast_to(part[None], (n, *part.shape))
    return lax.all_to_all(copies, axes, 0, 0, axis_index_groups=groups, tiled=True)


def solution(mesh):
    in_specs = (P(None, "gz", "gy", None), P("gz", "gy", None))
    out_specs = P(None, "gz", "gy", None)
    return jax.shard_map(shards, mesh=mesh, in_specs=in_specs, out_specs=out_specs, check_vma=False)
```
